128 devices in a mesh: sub: 32 (over x, z, core), help: 4 (over y).
Axes of the slice: x: 4, y: 4, z: 4, core: 2. Of those that a mesh axis runs over, the one named last changes fastest.
Arguments:
- right_side: float32 [32, 1024, 256], P('sub', 'help'), may hold values from -6 to 6
- operator_panels: bfloat16 [384, 128, 1536], P(('sub', 'help')), may hold values from -1 to 4, as said below
- panel_index: int32 [384], P(('sub', 'help')), may hold values from 0 to 11, as said below
- halo_map: int32 [32, 512], P('sub'), may hold values from 0 to 1023, as said below
- counts: int32 [32], P('sub'), may hold values from 512 to 1024
Outputs:
- solution: float32 [32, 1024, 256], P('sub', 'help')
- residual: float32 [32, 1024, 256], P('sub', 'help')
The draws below stay inside these ranges and needn't reach their ends.
Inputs may be any that keep to these rules, and one draw needn't show every extreme that they name: `panel_index`: within the 12 slots of one index of sub, every value appears exactly once. `halo_map`: the 512 entries of each subdomain are distinct; value v names row v of the subdomain of the previous index of sub. `operator_panels`: put in order, the 12 panels of each subdomain form a symmetric positive definite matrix.
All inputs are finite; a program needn't handle non-finite values.
Results may differ from the reference program's by a relative error of at most 0.023.
Values may be sent and summed in bfloat16 or wider, within the bound.
No kernel may reach another device: no remote copies, remote signals or barrier semaphores. Data moves between devices by JAX's collectives and lax.ppermute only.
A program may use at most 64 MiB of HBM per device.

```python
import math
import jax
import jax.numpy as jnp
from jax import lax

SUBS = 1
OWN = 1024
HALO = 512
PANEL = 128
RHS = 256
ITERS = 2
M = 1536
PANELS = 12
S = 32
N_SUB = 32


def group_orders(key):
    group_keys = jax.random.split(jax.random.fold_in(key, 11), N_SUB)
    return jax.vmap(lambda member: jax.random.permutation(member, SUBS * PANELS))(group_keys)


def draw_panel_index(key, part):
    return group_orders(key).reshape(-1).astype(jnp.int32)


def domain_operator(member):
    noise_key = jax.random.fold_in(member, 1)
    scale_key = jax.random.fold_in(member, 2)
    noise_block = jnp.clip(jax.random.normal(noise_key, (M, M), jnp.float32), -5.0, 5.0)
    symmetric = (noise_block + noise_block.T) * (0.3 / math.sqrt(2.0 * M))
    diagonal = jnp.exp(jax.random.uniform(scale_key, (M,), jnp.float32, 0.0, math.log(3.0)))
    return (symmetric + jnp.diag(diagonal)).astype(jnp.bfloat16)


def draw_operator_panels(key, part):
    base_key = jax.random.fold_in(key, 23)
    operators = lax.map(lambda domain_id: domain_operator(jax.random.fold_in(base_key, domain_id)), jnp.arange(S, dtype=jnp.int32))
    panel_rows = operators.reshape(S * PANELS, PANEL, M)
    offsets = (jnp.arange(N_SUB, dtype=jnp.int32) * (SUBS * PANELS))[:, None]
    return panel_rows[(group_orders(key) + offsets).reshape(-1)]


def draw_halo_map(key, part):
    group_keys = jax.random.split(jax.random.fold_in(key, 41), N_SUB)
    chosen = jax.vmap(lambda member: jax.random.permutation(member, SUBS * OWN)[:SUBS * HALO])(group_keys)
    return chosen.reshape(S, HALO).astype(jnp.int32)


def with_ends(values, own_key, smallest, high):
    longest = values.shape.index(max(values.shape))
    spots = []
    for shift in (0, 1):
        where = [jax.random.randint(jax.random.fold_in(own_key, axis), (), 0, length) for axis, length in enumerate(values.shape)]
        where[longest] = (where[longest] + shift) % values.shape[longest]
        spots.append(tuple(where))
    return values.at[spots[0]].set(smallest).at[spots[1]].set(high)


def level_of(rng, shape, shards, smallest, largest):
    factor_of, own = 1.0, jax.random.fold_in(rng, 6)
    for axis_at, parts in shards:
        draws = jnp.exp(jax.random.uniform(jax.random.fold_in(own, axis_at), (parts,), jnp.float32, smallest / len(shards), largest / len(shards)))
        factor_of = factor_of * jnp.repeat(draws, shape[axis_at] // parts).reshape([-1 if axis == axis_at else 1 for axis in range(len(shape))])
    return factor_of


def normal_values(stream_key, shape, deviation, most, cuts=(), kind=jnp.bfloat16):
    gain = level_of(stream_key, shape, cuts, -0.22, 0.18) if cuts else 1.0
    result = jax.random.normal(stream_key, shape, jnp.float32) * deviation * gain
    return jnp.minimum(jnp.maximum(result, -most), most).astype(kind)


def setup_inputs(seed: int = 0) -> dict:
    arg_keys = jax.random.split(jax.random.key(seed), 6)
    return {
        "right_side": normal_values(arg_keys[0], (S, OWN, RHS), 1.0, 6.0, ((0, 32), (1, 4)), jnp.float32),
        "operator_panels": draw_operator_panels(jax.random.fold_in(arg_keys[5], 71), 0),
        "panel_index": draw_panel_index(jax.random.fold_in(arg_keys[5], 71), 0),
        "halo_map": draw_halo_map(jax.random.fold_in(arg_keys[5], 71), 0),
        "counts": with_ends(jax.random.randint(arg_keys[4], (S,), OWN // 2, OWN + 1), jax.random.fold_in(arg_keys[4], 1), OWN // 2, OWN).astype(jnp.int32),
    }


def spd_solve(matrix, targets):
    factor = jnp.linalg.cholesky(matrix)
    return jax.scipy.linalg.cho_solve((factor, True), targets)

def inner(left_block, right_block):
    return jnp.einsum('nr,ns->rs', left_block.reshape(-1, RHS), right_block.reshape(-1, RHS), precision=lax.Precision.HIGHEST)

def times(state_block, weights_mix):
    return jnp.dot(state_block, weights_mix, precision=lax.Precision.HIGHEST)

def take_rows(source, where):
    return jnp.take(source, where, axis=0)

def add_back(halo_vals, where):
    return jnp.zeros((SUBS * OWN, RHS), jnp.float32).at[where].add(-halo_vals)

def apply_operator(direction, operator_panels, slot_domain, slot_panel, group_maps, live_mask):
    lowered = direction.astype(jnp.bfloat16)
    groups = lowered.reshape(N_SUB, SUBS * OWN, RHS)
    previous = jnp.concatenate([jnp.zeros((1, SUBS * OWN, RHS), jnp.bfloat16), groups[:-1]], axis=0)
    borrowed = jax.vmap(take_rows)(previous, group_maps)
    local_block = jnp.concatenate([lowered, -borrowed.reshape(S, HALO, RHS)], axis=1)

    def one_panel(slot_index):
        domain_block = local_block[slot_domain[slot_index]]
        return jnp.dot(operator_panels[slot_index].astype(jnp.float32), domain_block.astype(jnp.float32), preferred_element_type=jnp.float32).astype(jnp.bfloat16)
    products = lax.map(one_panel, jnp.arange(S * PANELS, dtype=jnp.int32))
    placed = jnp.zeros((S * PANELS, PANEL, RHS), jnp.bfloat16).at[slot_domain * PANELS + slot_panel].set(products)
    placed = placed.reshape(S, M, RHS)
    own_out = placed[:, :OWN].astype(jnp.float32)
    halo_out = placed[:, OWN:].astype(jnp.float32).reshape(N_SUB, SUBS * HALO, RHS)
    back_terms = jax.vmap(add_back)(halo_out, group_maps)
    received = jnp.concatenate([back_terms[1:], jnp.zeros((1, SUBS * OWN, RHS), jnp.float32)], axis=0)
    return (own_out + received.reshape(S, OWN, RHS)) * live_mask

def reference(right_side, operator_panels, panel_index, halo_map, counts):
    live_mask = (jnp.arange(OWN, dtype=jnp.int32)[None, :] < counts[:, None]).astype(jnp.float32)[:, :, None]
    group_ids = jnp.arange(S * PANELS, dtype=jnp.int32) // (SUBS * PANELS)
    slot_domain = (group_ids * SUBS + panel_index // PANELS).astype(jnp.int32)
    slot_panel = (panel_index % PANELS).astype(jnp.int32)
    group_maps = halo_map.reshape(N_SUB, SUBS * HALO).astype(jnp.int32)
    residual = right_side * live_mask
    solution = jnp.zeros_like(residual)
    direction = residual
    norm_now = inner(residual, residual)
    for iteration in range(ITERS):
        applied = apply_operator(direction, operator_panels, slot_domain, slot_panel, group_maps, live_mask)
        step_size = spd_solve(inner(direction, applied), norm_now)
        solution = solution + times(direction, step_size)
        residual = residual - times(applied, step_size)
        if iteration + 1 < ITERS:
            norm_next = inner(residual, residual)
            step_mix = spd_solve(norm_now, norm_next)
            direction = residual + times(direction, step_mix)
            norm_now = norm_next
    return (solution, residual)
```

```python
import jax
import jax.numpy as jnp
from jax import lax
from jax.experimental import pallas as pl
from jax.experimental.pallas import tpu as pltpu
from jax.sharding import Mesh
from jax.sharding import PartitionSpec as P

SUB = ("sub_0", "sub_1", "sub_2")
SUB_HELP = ("sub_0", "sub_1", "sub_2", "help")
SHIFT = 3.0
BF = jnp.bfloat16
F32 = jnp.float32


def shifted(value, axis, by):
    devices = lax.axis_size(axis)
    pairs = [(i, i + by) for i in range(devices) if 0 <= i + by < devices]
    return lax.ppermute(value, axis, pairs)


def turned(value, axis, by):
    devices = lax.axis_size(axis)
    return lax.ppermute(value, axis, [(i, (i + by) % devices) for i in range(devices)])


def from_others(value, axis):
    return [turned(value, axis, by) for by in range(1, lax.axis_size(axis))]


def summed(value, axis):
    total = value
    for other in from_others(value, axis):
        total = total + other
    return total


def whole(space=None):
    return pl.BlockSpec(memory_space=pltpu.MemorySpace.VMEM if space is None else space)


def scalars():
    return pl.BlockSpec(memory_space=pltpu.MemorySpace.SMEM)


def call(body, args, outs, scratch=(), small=1, name=None):
    specs = [scalars()] * small + [whole()] * (len(args) - small)
    return pl.pallas_call(
        body,
        in_specs=specs,
        out_specs=[whole() for _ in outs],
        out_shape=[jax.ShapeDtypeStruct(s, d) for s, d in outs],
        scratch_shapes=list(scratch),
        name=name,
    )(*args)


def iota(shape, dim):
    return lax.broadcasted_iota(jnp.int32, shape, dim)


def mm(a, b):
    return lax.dot_general(a, b, (((1,), (0,)), ((), ())), preferred_element_type=F32)


def tmm(a, b):
    return lax.dot_general(a, b, (((0,), (0,)), ((), ())), preferred_element_type=F32)


def halves(a):
    high = a.astype(BF)
    return high, (a - high.astype(F32)).astype(BF)


def mm3(a, b):
    ah, al = halves(a)
    bh, bl = halves(b)
    return mm(ah, bh) + (mm(ah, bl) + mm(al, bh))


def mmf(a, b):
    return jnp.dot(a, b, precision=lax.Precision.HIGHEST, preferred_element_type=F32)


def hot(mask):
    return jnp.where(mask, 1.0, 0.0).astype(BF)


def lower_body(sc, r_ref, out_ref):
    rows = r_ref.shape[0]
    cols = r_ref.shape[1]
    row = iota((rows, 1), 0) + sc[0] * rows
    live = row < sc[1]
    out_ref[:rows, :] = jnp.where(live, r_ref[...], 0.0).astype(BF)
    col = iota((16, cols), 1)
    info = jnp.zeros((16, cols), F32)
    values = [sc[3], sc[4], sc[5], sc[1] // 32, sc[1] % 32]
    for k, value in enumerate(values):
        info = jnp.where(col == k, value.astype(F32), info)
    out_ref[rows:, :] = info.astype(BF)


def pick_body(sc, own_ref, a_ref, b_ref, c_ref, later_ref, wg_ref, pick_ref):
    rows = own_ref.shape[0] - 16
    h = sc[0]
    for k, ref in enumerate((own_ref, a_ref, b_ref, c_ref)):
        at = pl.multiple_of(lax.rem(h + 4 - k, 4) * rows, rows)
        wg_ref[pl.ds(at, rows), :] = ref[:rows, :]
    halo = later_ref.shape[0]
    choose = hot(later_ref[...] == iota((halo, wg_ref.shape[0]), 1))
    pick_ref[:halo, :] = mm(choose, wg_ref[...]).astype(BF)
    pick_ref[halo:, :] = own_ref[rows:, :]


def first_body(f_ref, wg_ref, halo_ref, z_ref):
    owned = wg_ref.shape[0]
    halo = f_ref.shape[1] - owned
    z = mm(f_ref[:, :owned], wg_ref[...]) - mm(f_ref[:, owned:], halo_ref[:halo, :])
    z_ref[...] = z.astype(BF)


def spread_body(sc, own_ref, a_ref, b_ref, c_ref, later_ref, zg_ref, halo_ref, pick_ref):
    panel = own_ref.shape[0] // 3
    for k, ref in enumerate((own_ref, a_ref, b_ref, c_ref)):
        for j in range(3):
            at = pl.multiple_of(sc[3 + 3 * k + j] * panel, panel)
            zg_ref[pl.ds(at, panel), :] = ref[j * panel : (j + 1) * panel, :]
    halo = halo_ref.shape[0]
    owned = zg_ref.shape[0] - halo
    halo_ref[...] = zg_ref[owned:, :]
    later = later_ref[...]
    choose = hot((later == iota((halo, owned), 1)) & (later < sc[1]))
    pick_ref[...] = mm(choose, zg_ref[:owned, :]).astype(BF)


def second_body(
    sc, f_ref, zg_ref, ret_ref, zp_ref, bor_ref, wg_ref, map_ref, later_ref, z_ref, im_ref, vb_ref, vh_ref
):
    owned = wg_ref.shape[0]
    halo = ret_ref.shape[0]
    live = iota((owned, 1), 0) < sc[1]
    back = mm(hot(iota((owned, halo), 0) == later_ref[...]), ret_ref[...])
    image = jnp.where(live, zg_ref[:owned, :].astype(F32) - back, 0.0)
    im_ref[...] = image
    vb = (image - SHIFT * wg_ref[...].astype(F32)).astype(BF)
    vb_ref[...] = vb
    info = bor_ref[halo : halo + 1, :].astype(F32)
    lane = iota(info.shape, 1)
    weight = jnp.where(lane == 3, 32.0, jnp.where(lane == 4, 1.0, 0.0))
    count = jnp.sum(info * weight, axis=1, keepdims=True)
    alive = (map_ref[...].astype(F32) < count) & (sc[2] > 0)
    term = zp_ref[...].astype(F32) - zg_ref[owned:, :].astype(F32)
    vh = jnp.where(alive, term, 0.0) - SHIFT * bor_ref[:halo, :].astype(F32)
    vh = vh.astype(BF)
    vh_ref[...] = vh
    z = mm(f_ref[:, :owned], vb) - mm(f_ref[:, owned:], vh)
    z_ref[...] = z.astype(BF)


def gram_body(
    sc, own_ref, a_ref, b_ref, c_ref, wg_ref, bor_ref, zg_ref, im_ref, vb_ref, vh_ref, map_ref,
    pack_ref, back_ref, mine_ref, z2_ref, gram_ref,
):
    panel = own_ref.shape[0] // 3
    for k, ref in enumerate((own_ref, a_ref, b_ref, c_ref)):
        for j in range(3):
            at = pl.multiple_of(sc[3 + 3 * k + j] * panel, panel)
            z2_ref[pl.ds(at, panel), :] = ref[j * panel : (j + 1) * panel, :]
    owned = wg_ref.shape[0]
    halo = vh_ref.shape[0]
    rows = mine_ref.shape[0]
    h = sc[0]
    at = pl.multiple_of(h * rows, rows)
    mine_ref[...] = z2_ref[pl.ds(at, rows), :]
    choose = hot(iota((rows, halo), 0) + h * rows == map_ref[...])
    back_ref[...] = mm(choose, z2_ref[owned:, :]).astype(BF)

    @pl.when(h == 0)
    def _():
        gram_ref[...] = tmm(wg_ref[...], wg_ref[...])

    @pl.when(h == 1)
    def _():
        gram_ref[...] = tmm(wg_ref[...], zg_ref[:owned, :]) - tmm(bor_ref[:halo, :], zg_ref[owned:, :])

    @pl.when(h == 2)
    def _():
        high, low = halves(im_ref[...])
        cross = tmm(low, high)
        gram_ref[...] = tmm(high, high) + (cross + cross.T)

    @pl.when(h == 3)
    def _():
        gram_ref[...] = tmm(vb_ref[...], z2_ref[:owned, :]) - tmm(vh_ref[...], z2_ref[owned:, :])

    half = gram_ref.shape[0] // 2
    lower = gram_ref[:half, :half]
    upper = gram_ref[half:, half:]
    r, c = iota((half, half), 0), iota((half, half), 1)
    pack_ref[:half, :] = jnp.where(r >= c, lower, upper.T)
    pack_ref[half : 2 * half, :] = gram_ref[half:, :half]
    diagonal = jnp.sum(jnp.where(r == c, upper, 0.0), axis=0, keepdims=True)
    pack_ref[2 * half :, :] = jnp.broadcast_to(diagonal, (8, half))


def unpacked(pack, out_ref):
    half = pack.shape[1]
    r, c = iota((half, half), 0), iota((half, half), 1)
    both = pack[:half, :]
    flip = both.T
    side = pack[half : 2 * half, :]
    out_ref[:half, :half] = jnp.where(r >= c, both, flip)
    out_ref[half:, half:] = jnp.where(r == c, pack[2 * half : 2 * half + 1, :], jnp.where(r < c, both, flip))
    out_ref[half:, :half] = side
    out_ref[:half, half:] = side.T


def inverse(k, x_ref):
    n = k.shape[0]
    r, c = iota((n, n), 0), iota((n, n), 1)
    eye = jnp.where(r == c, 1.0, 0.0)
    on = jnp.where(r == c, k, 0.0)
    by_row = lax.rsqrt(jnp.sum(on, axis=1, keepdims=True))
    by_col = lax.rsqrt(jnp.sum(on, axis=0, keepdims=True))
    unit = k * by_row * by_col
    norm = jnp.max(jnp.sum(jnp.abs(unit), axis=0, keepdims=True), axis=1, keepdims=True)
    step = 2.0 / (1.0 + norm)
    x_ref[...] = step * (2.0 * eye - step * unit)

    def more(state):
        return (state[0] < 60) & (state[1] > 1e-3)

    def improve(state):
        x = x_ref[...]
        left = eye - mmf(unit, x)
        x_ref[...] = x + mmf(x, left)
        return state[0] + 1, jnp.max(jnp.sum(jnp.abs(left), axis=0, keepdims=True))

    lax.while_loop(more, improve, (jnp.int32(0), jnp.float32(1.0)))
    return x_ref[...] * by_row * by_col


def solve_body(
    sc, own_ref, a_ref, b_ref, c_ref, r_ref, im_ref, w_ref, mine_ref, ret_ref,
    sol_ref, res_ref, pack_ref, g00_ref, g01_ref, g11_ref, gvv_ref, x_ref,
):
    h = sc[0]
    for k, ref in enumerate((own_ref, a_ref, b_ref, c_ref)):
        pack_ref[lax.rem(h + 4 - k, 4)] = ref[...]
    for k, ref in enumerate((g00_ref, g01_ref, g11_ref, gvv_ref)):
        unpacked(pack_ref[k], ref)
    g01 = g01_ref[...]
    mixed = g11_ref[...] - SHIFT * g01
    inv = inverse(g01, x_ref)
    p1 = mmf(inv, mixed)
    p2 = mmf(inv, g00_ref[...])
    schur = gvv_ref[...] - mmf(mixed, p1)
    schur = 0.5 * (schur + schur.T)
    rest = g01 - SHIFT * g00_ref[...] - mmf(mixed, p2)
    cv = mmf(inverse(schur, x_ref), rest)
    cr = p2 - mmf(p1, cv)
    rows = r_ref.shape[0]
    live = iota((rows, 1), 0) + h * rows < sc[1]
    r = jnp.where(live, r_ref[...], 0.0)
    at = pl.multiple_of(h * rows, rows)
    im = im_ref[pl.ds(at, rows), :]
    v = im - SHIFT * w_ref[:rows, :].astype(F32)
    av = jnp.where(live, mine_ref[...].astype(F32) - ret_ref[...].astype(F32), 0.0)
    sol_ref[...] = mm3(r, cr) + mm3(v, cv)
    res_ref[...] = r - mm3(im, cr) - mm3(av, cv)


def shards(right_side, operator_panels, panel_index, halo_map, counts):
    rows, cols = right_side.shape[1:]
    slots, panel, wide = operator_panels.shape
    halo = halo_map.shape[1]
    owned = rows * lax.axis_size("help")
    helper = lax.axis_index("help").astype(jnp.int32)
    group = lax.axis_index(SUB).astype(jnp.int32)
    r = right_side.reshape(rows, cols)
    f = operator_panels.reshape(slots * panel, wide)
    head = jnp.stack([helper, counts[0], (group > 0).astype(jnp.int32)])
    sc = jnp.concatenate([head, panel_index])
    later = shifted(halo_map.reshape(halo), SUB, -1)
    later_col, later_row = later.reshape(halo, 1), later.reshape(1, halo)
    map_col, map_row = halo_map.reshape(halo, 1), halo_map.reshape(1, halo)

    (low,) = call(lower_body, (sc, r), [((rows + 16, cols), BF)], name="lower")
    others = from_others(low, "help")
    tables = [o[rows, :slots].astype(jnp.int32) for o in others]
    sc = jnp.concatenate([sc, *tables])
    wg, pick = call(
        pick_body, (sc, low, *others, later_col), [((owned, cols), BF), ((halo + 16, cols), BF)], name="pick"
    )
    bor = shifted(pick, SUB, 1)
    (z,) = call(first_body, (f, wg, bor), [((slots * panel, cols), BF)], small=0, name="first")
    zs = from_others(z, "help")
    zg, zh, zpick = call(
        spread_body,
        (sc, z, *zs, later_col),
        [((wide, cols), BF), ((halo, cols), BF), ((halo, cols), BF)],
        name="spread",
    )
    ret = shifted(zh, SUB, -1)
    zp = shifted(zpick, SUB, 1)
    z2, im, vb, vh = call(
        second_body,
        (sc, f, zg, ret, zp, bor, wg, map_col, later_row),
        [((slots * panel, cols), BF), ((owned, cols), F32), ((owned, cols), BF), ((halo, cols), BF)],
        name="second",
    )
    z2s = from_others(z2, "help")
    pack, back, mine = call(
        gram_body,
        (sc, z2, *z2s, wg, bor, zg, im, vb, vh, map_row),
        [((cols + 8, cols // 2), F32), ((rows, cols), BF), ((rows, cols), BF)],
        scratch=[pltpu.VMEM((wide, cols), BF), pltpu.VMEM((cols, cols), F32)],
        name="gram",
    )
    ret2 = shifted(back, SUB, -1)
    pack = summed(pack, "sub_2")
    pack = summed(pack, "sub_0")
    pack = summed(pack, "sub_1")
    packs = from_others(pack, "help")
    sol, res = call(
        solve_body,
        (sc, pack, *packs, r, im, low, mine, ret2),
        [((rows, cols), F32), ((rows, cols), F32)],
        scratch=[pltpu.VMEM((4, cols + 8, cols // 2), F32)] + [pltpu.VMEM((cols, cols), F32)] * 5,
        name="solve",
    )
    return sol.reshape(right_side.shape), res.reshape(right_side.shape)


def solution(mesh):
    torus = Mesh(
        mesh.devices.reshape(4, 4, 2, mesh.shape["help"]), ("sub_0", "sub_1", "sub_2", "help")
    )
    in_specs = (P(SUB, "help", None), P(SUB_HELP, None, None), P(SUB_HELP), P(SUB, None), P(SUB))
    out_specs = (P(SUB, "help", None), P(SUB, "help", None))
    return jax.shard_map(
        shards, mesh=torus, in_specs=in_specs, out_specs=out_specs, check_vma=False
    )
```

```python
import jax
import jax.numpy as jnp
from jax import lax
from jax.experimental import pallas as pl
from jax.experimental.pallas import tpu as pltpu
from jax.sharding import Mesh
from jax.sharding import PartitionSpec as P

SUB = ("sub_0", "sub_1", "sub_2")
SUB_HELP = ("sub_0", "sub_1", "sub_2", "help")
SHIFT = 3.0
BF = jnp.bfloat16
F32 = jnp.float32


def shifted(value, axis, by):
    devices = lax.axis_size(axis)
    pairs = [(i, i + by) for i in range(devices) if 0 <= i + by < devices]
    return lax.ppermute(value, axis, pairs)


def turned(value, axis, by):
    devices = lax.axis_size(axis)
    return lax.ppermute(value, axis, [(i, (i + by) % devices) for i in range(devices)])


def from_others(value, axis):
    return [turned(value, axis, by) for by in range(1, lax.axis_size(axis))]


def summed(value, axis):
    total = value
    for other in from_others(value, axis):
        total = total + other
    return total


def whole(space=None):
    return pl.BlockSpec(memory_space=pltpu.MemorySpace.VMEM if space is None else space)


def scalars():
    return pl.BlockSpec(memory_space=pltpu.MemorySpace.SMEM)


def call(body, args, outs, scratch=(), small=1, name=None):
    specs = [scalars()] * small + [whole()] * (len(args) - small)
    return pl.pallas_call(
        body,
        in_specs=specs,
        out_specs=[whole() for _ in outs],
        out_shape=[jax.ShapeDtypeStruct(s, d) for s, d in outs],
        scratch_shapes=list(scratch),
        compiler_params=pltpu.CompilerParams(vmem_limit_bytes=16 << 20),
        name=name,
    )(*args)


def iota(shape, dim):
    return lax.broadcasted_iota(jnp.int32, shape, dim)


def mm(a, b):
    return lax.dot_general(a, b, (((1,), (0,)), ((), ())), preferred_element_type=F32)


def tmm(a, b):
    return lax.dot_general(a, b, (((0,), (0,)), ((), ())), preferred_element_type=F32)


def halves(a):
    high = a.astype(BF)
    return high, (a - high.astype(F32)).astype(BF)


def mm3(a, b):
    ah, al = halves(a)
    bh, bl = halves(b)
    return mm(ah, bh) + (mm(ah, bl) + mm(al, bh))


def mmf(a, b):
    return jnp.dot(a, b, precision=lax.Precision.HIGHEST, preferred_element_type=F32)


def hot(mask):
    return jnp.where(mask, 1.0, 0.0).astype(BF)


def here():
    return lax.axis_index("help")


def lower_body(count, index, r_ref, out_ref):
    rows = r_ref.shape[0]
    cols = r_ref.shape[1]
    row = iota((rows, 1), 0) + here() * rows
    out_ref[:rows, :] = jnp.where(row < count[0], r_ref[...], 0.0).astype(BF)
    col = iota((16, cols), 1)
    info = jnp.zeros((16, cols), F32)
    values = [index[0], index[1], index[2], count[0] // 32, count[0] % 32]
    for k, value in enumerate(values):
        info = jnp.where(col == k, value.astype(F32), info)
    out_ref[rows:, :] = info.astype(BF)


def pick_body(own_ref, a_ref, b_ref, c_ref, later_ref, wg_ref, pick_ref):
    rows = own_ref.shape[0] - 16
    h = here()
    for k, ref in enumerate((own_ref, a_ref, b_ref, c_ref)):
        at = pl.multiple_of(lax.rem(h + 4 - k, 4) * rows, rows)
        wg_ref[pl.ds(at, rows), :] = ref[:rows, :]
    halo = later_ref.shape[0]
    choose = hot(later_ref[...] == iota((halo, wg_ref.shape[0]), 1))
    pick_ref[:halo, :] = mm(choose, wg_ref[...]).astype(BF)
    pick_ref[halo:, :] = own_ref[rows:, :]


def early_body(f_ref, wg_ref, z_ref):
    z_ref[...] = mm(f_ref[:, : wg_ref.shape[0]], wg_ref[...])


def first_body(f_ref, early_ref, halo_ref, z_ref):
    halo = halo_ref.shape[0] - 16
    owned = f_ref.shape[1] - halo
    z_ref[...] = (early_ref[...] - mm(f_ref[:, owned:], halo_ref[:halo, :])).astype(BF)


def spread_body(count, index, own_ref, a_ref, b_ref, c_ref, later_ref, zg_ref, halo_ref, pick_ref):
    panel = own_ref.shape[0] // 3
    for k, ref in enumerate((own_ref, a_ref, b_ref, c_ref)):
        for j in range(3):
            at = pl.multiple_of(index[3 * k + j] * panel, panel)
            zg_ref[pl.ds(at, panel), :] = ref[j * panel : (j + 1) * panel, :]
    halo = halo_ref.shape[0]
    owned = zg_ref.shape[0] - halo
    halo_ref[...] = zg_ref[owned:, :]
    later = later_ref[...]
    choose = hot((later == iota((halo, owned), 1)) & (later < count[0]))
    pick_ref[...] = mm(choose, zg_ref[:owned, :]).astype(BF)


def second_body(
    count, f_ref, zg_ref, ret_ref, zp_ref, bor_ref, wg_ref, map_ref, later_ref, z_ref, im_ref, vb_ref, vh_ref
):
    owned = wg_ref.shape[0]
    halo = ret_ref.shape[0]
    live = iota((owned, 1), 0) < count[0]
    back = mm(hot(iota((owned, halo), 0) == later_ref[...]), ret_ref[...])
    image = jnp.where(live, zg_ref[:owned, :].astype(F32) - back, 0.0)
    im_ref[...] = image
    vb = (image - SHIFT * wg_ref[...].astype(F32)).astype(BF)
    vb_ref[...] = vb
    info = bor_ref[halo : halo + 1, :].astype(F32)
    lane = iota(info.shape, 1)
    weight = jnp.where(lane == 3, 32.0, jnp.where(lane == 4, 1.0, 0.0))
    before = jnp.sum(info * weight, axis=1, keepdims=True)
    alive = (map_ref[...].astype(F32) < before) & (lax.axis_index(SUB) > 0)
    term = zp_ref[...].astype(F32) - zg_ref[owned:, :].astype(F32)
    vh = jnp.where(alive, term, 0.0) - SHIFT * bor_ref[:halo, :].astype(F32)
    vh = vh.astype(BF)
    vh_ref[...] = vh
    z = mm(f_ref[:, :owned], vb) - mm(f_ref[:, owned:], vh)
    z_ref[...] = z.astype(BF)


def gram_body(
    index, own_ref, a_ref, b_ref, c_ref, wg_ref, bor_ref, zg_ref, im_ref, vb_ref, vh_ref,
    keep_ref, give_ref, z2_ref, gram_ref, pack_ref,
):
    panel = own_ref.shape[0] // 3
    for k, ref in enumerate((own_ref, a_ref, b_ref, c_ref)):
        for j in range(3):
            at = pl.multiple_of(index[3 * k + j] * panel, panel)
            z2_ref[pl.ds(at, panel), :] = ref[j * panel : (j + 1) * panel, :]
    owned = wg_ref.shape[0]
    halo = vh_ref.shape[0]
    h = here()

    @pl.when(h == 0)
    def _():
        gram_ref[...] = tmm(wg_ref[...], wg_ref[...])

    @pl.when(h == 1)
    def _():
        gram_ref[...] = tmm(wg_ref[...], zg_ref[:owned, :]) - tmm(bor_ref[:halo, :], zg_ref[owned:, :])

    @pl.when(h == 2)
    def _():
        high, low = halves(im_ref[...])
        cross = tmm(low, high)
        gram_ref[...] = tmm(high, high) + (cross + cross.T)

    @pl.when(h == 3)
    def _():
        gram_ref[...] = tmm(vb_ref[...], z2_ref[:owned, :]) - tmm(vh_ref[...], z2_ref[owned:, :])

    half = gram_ref.shape[0] // 2
    lower = gram_ref[:half, :half]
    upper = gram_ref[half:, half:]
    r, c = iota((half, half), 0), iota((half, half), 1)
    diagonal = jnp.sum(jnp.where(r == c, upper, 0.0), axis=0, keepdims=True)
    pack_ref[0, :half, :] = jnp.where(r >= c, lower, upper.T)
    pack_ref[1, :half, :] = gram_ref[half:, :half]
    pack_ref[0, half:, :] = jnp.broadcast_to(diagonal, (8, half))
    pack_ref[1, half:, :] = jnp.zeros((8, half), F32)
    core = lax.axis_index("sub_2")
    keep_ref[...] = pack_ref[core]
    give_ref[...] = pack_ref[1 - core]


def tail_body(z_ref, map_ref, mine_ref, back_ref):
    rows = mine_ref.shape[0]
    halo = map_ref.shape[1]
    at = pl.multiple_of(here() * rows, rows)
    mine_ref[...] = z_ref[pl.ds(at, rows), :]
    choose = hot(iota((rows, halo), 0) + at == map_ref[...])
    back_ref[...] = mm(choose, z_ref[z_ref.shape[0] - halo :, :]).astype(BF)


def unpacked(pack, out_ref):
    half = pack.shape[2]
    r, c = iota((half, half), 0), iota((half, half), 1)
    both = pack[0, :half, :]
    flip = both.T
    side = pack[1, :half, :]
    out_ref[:half, :half] = jnp.where(r >= c, both, flip)
    out_ref[half:, half:] = jnp.where(r == c, pack[0, half : half + 1, :], jnp.where(r < c, both, flip))
    out_ref[half:, :half] = side
    out_ref[:half, half:] = side.T


def inverse(k, x_ref):
    n = k.shape[0]
    r, c = iota((n, n), 0), iota((n, n), 1)
    eye = jnp.where(r == c, 1.0, 0.0)
    on = jnp.where(r == c, k, 0.0)
    by_row = lax.rsqrt(jnp.sum(on, axis=1, keepdims=True))
    by_col = lax.rsqrt(jnp.sum(on, axis=0, keepdims=True))
    unit = k * by_row * by_col
    norm = jnp.max(jnp.sum(jnp.abs(unit), axis=0, keepdims=True), axis=1, keepdims=True)
    step = 2.0 / (1.0 + norm)
    high, low = halves(unit)
    x = 2.0 * eye - unit
    left = eye - mm(high, x.astype(BF))
    for _ in range(2):
        x = x + mm(x.astype(BF), left.astype(BF))
        xh, xl = halves(x)
        left = eye - (mm(high, xh) + (mm(high, xl) + mm(low, xh)))
    x_ref[...] = x + mm(x.astype(BF), left.astype(BF))

    def size(error):
        return jnp.max(jnp.sum(jnp.abs(error), axis=0, keepdims=True))

    @pl.when(jnp.logical_not(size(left) < 3e-3))
    def _():
        x_ref[...] = step * eye

        def more(state):
            return (state[0] < 60) & (state[1] > 1e-3)

        def improve(state):
            x = x_ref[...]
            left = eye - mmf(unit, x)
            x_ref[...] = x + mmf(x, left)
            return state[0] + 1, size(left)

        lax.while_loop(more, improve, (jnp.int32(0), jnp.float32(1.0)))

    return x_ref[...] * by_row * by_col


def solve_body(
    count, own_ref, a_ref, b_ref, c_ref, r_ref, im_ref, w_ref, mine_ref, ret_ref,
    sol_ref, res_ref, pack_ref, g00_ref, g01_ref, g11_ref, gvv_ref, x_ref,
):
    h = here()
    core = lax.axis_index("sub_2")
    for k, ref in enumerate((own_ref, a_ref, b_ref, c_ref)):
        at = lax.rem(h + 4 - k, 4)
        pack_ref[at, core] = ref[0]
        pack_ref[at, 1 - core] = ref[1]
    for k, ref in enumerate((g00_ref, g01_ref, g11_ref, gvv_ref)):
        unpacked(pack_ref.at[k], ref)
    g01 = g01_ref[...]
    mixed = g11_ref[...] - SHIFT * g01
    inv = inverse(g01, x_ref)
    p1 = mm3(inv, mixed)
    p2 = mm3(inv, g00_ref[...])
    schur = gvv_ref[...] - mm3(mixed, p1)
    schur = 0.5 * (schur + schur.T)
    rest = g01 - SHIFT * g00_ref[...] - mm3(mixed, p2)
    cv = mm3(inverse(schur, x_ref), rest)
    cr = p2 - mm3(p1, cv)
    rows = r_ref.shape[0]
    live = iota((rows, 1), 0) + h * rows < count[0]
    r = jnp.where(live, r_ref[...], 0.0)
    at = pl.multiple_of(h * rows, rows)
    im = im_ref[pl.ds(at, rows), :]
    v = im - SHIFT * w_ref[:rows, :].astype(F32)
    av = jnp.where(live, mine_ref[...].astype(F32) - ret_ref[...].astype(F32), 0.0)
    sol_ref[...] = mm3(r, cr) + mm3(v, cv)
    res_ref[...] = r - mm3(im, cr) - mm3(av, cv)


def shards(right_side, operator_panels, panel_index, halo_map, counts):
    rows, cols = right_side.shape[1:]
    slots, panel, wide = operator_panels.shape
    halo = halo_map.shape[1]
    half = cols // 2
    owned = rows * lax.axis_size("help")
    r = right_side.reshape(rows, cols)
    f = operator_panels.reshape(slots * panel, wide)
    later = shifted(halo_map.reshape(halo), SUB, -1)
    later_col, later_row = later.reshape(halo, 1), later.reshape(1, halo)
    map_col, map_row = halo_map.reshape(halo, 1), halo_map.reshape(1, halo)

    (low,) = call(lower_body, (counts, panel_index, r), [((rows + 16, cols), BF)], small=2, name="lower")
    others = from_others(low, "help")
    wg, pick = call(
        pick_body,
        (low, *others, later_col),
        [((owned, cols), BF), ((halo + 16, cols), BF)],
        small=0,
        name="pick",
    )
    bor = shifted(pick, SUB, 1)
    (early,) = call(early_body, (f, wg), [((slots * panel, cols), F32)], small=0, name="early")
    index = jnp.concatenate([panel_index, *(o[rows, :slots].astype(jnp.int32) for o in others)])
    (z,) = call(first_body, (f, early, bor), [((slots * panel, cols), BF)], small=0, name="first")
    zs = from_others(z, "help")
    zg, zh, zpick = call(
        spread_body,
        (counts, index, z, *zs, later_col),
        [((wide, cols), BF), ((halo, cols), BF), ((halo, cols), BF)],
        small=2,
        name="spread",
    )
    ret = shifted(zh, SUB, -1)
    zp = shifted(zpick, SUB, 1)
    z2, im, vb, vh = call(
        second_body,
        (counts, f, zg, ret, zp, bor, wg, map_col, later_row),
        [((slots * panel, cols), BF), ((owned, cols), F32), ((owned, cols), BF), ((halo, cols), BF)],
        name="second",
    )
    z2s = from_others(z2, "help")
    keep, give, z2g = call(
        gram_body,
        (index, z2, *z2s, wg, bor, zg, im, vb, vh),
        [((half + 8, half), F32), ((half + 8, half), F32), ((wide, cols), BF)],
        scratch=[pltpu.VMEM((cols, cols), F32), pltpu.VMEM((2, half + 8, half), F32)],
        name="gram",
    )
    pack = keep + turned(give, "sub_2", 1)
    mine, back = call(
        tail_body, (z2g, map_row), [((rows, cols), BF), ((rows, cols), BF)], small=0, name="tail"
    )
    ret2 = shifted(back, SUB, -1)
    pack = summed(pack, "sub_0")
    pack = summed(pack, "sub_1")
    pack = jnp.stack([pack, turned(pack, "sub_2", 1)])
    packs = from_others(pack, "help")
    sol, res = call(
        solve_body,
        (counts, pack, *packs, r, im, low, mine, ret2),
        [((rows, cols), F32), ((rows, cols), F32)],
        scratch=[pltpu.VMEM((4, 2, half + 8, half), F32)] + [pltpu.VMEM((cols, cols), F32)] * 5,
        name="solve",
    )
    return sol.reshape(right_side.shape), res.reshape(right_side.shape)


def solution(mesh):
    torus = Mesh(
        mesh.devices.reshape(4, 4, 2, mesh.shape["help"]), ("sub_0", "sub_1", "sub_2", "help")
    )
    in_specs = (P(SUB, "help", None), P(SUB_HELP, None, None), P(SUB_HELP), P(SUB, None), P(SUB))
    out_specs = (P(SUB, "help", None), P(SUB, "help", None))
    return jax.shard_map(
        shards, mesh=torus, in_specs=in_specs, out_specs=out_specs, check_vma=False
    )
```

```python
import jax
import jax.numpy as jnp
from jax import lax
from jax.experimental import pallas as pl
from jax.experimental.pallas import tpu as pltpu
from jax.sharding import Mesh
from jax.sharding import PartitionSpec as P

SUB = ("sub_0", "sub_1", "sub_2")
SUB_HELP = ("sub_0", "sub_1", "sub_2", "help")
SHIFT = 3.0
BF = jnp.bfloat16
F32 = jnp.float32


def turned(value, axis, by):
    devices = lax.axis_size(axis)
    return lax.ppermute(value, axis, [(i, (i + by) % devices) for i in range(devices)])


def from_others(value, axis):
    return [turned(value, axis, by) for by in range(1, lax.axis_size(axis))]


def summed(value, axis):
    total = value
    for other in from_others(value, axis):
        total = total + other
    return total


def whole(space=None):
    return pl.BlockSpec(memory_space=pltpu.MemorySpace.VMEM if space is None else space)


def scalars():
    return pl.BlockSpec(memory_space=pltpu.MemorySpace.SMEM)


def call(body, args, outs, scratch=(), small=1, name=None, tail=None):
    specs = [scalars()] * small + [whole()] * (len(args) - small)
    return pl.pallas_call(
        body,
        in_specs=specs,
        out_specs=[whole() for _ in outs[1:]] + [tail or whole()],
        out_shape=[jax.ShapeDtypeStruct(s, d) for s, d in outs],
        scratch_shapes=list(scratch),
        compiler_params=pltpu.CompilerParams(vmem_limit_bytes=16 << 20),
        name=name,
    )(*args)


def iota(shape, dim):
    return lax.broadcasted_iota(jnp.int32, shape, dim)


def mm(a, b):
    return lax.dot_general(a, b, (((1,), (0,)), ((), ())), preferred_element_type=F32)


def tmm(a, b):
    return lax.dot_general(a, b, (((0,), (0,)), ((), ())), preferred_element_type=F32)


def halves(a):
    high = a.astype(BF)
    return high, (a - high.astype(F32)).astype(BF)


def mm3(a, b):
    ah, al = halves(a)
    bh, bl = halves(b)
    return mm(ah, bh) + (mm(ah, bl) + mm(al, bh))


def mmf(a, b):
    return jnp.dot(a, b, precision=lax.Precision.HIGHEST, preferred_element_type=F32)


def hot(mask):
    return jnp.where(mask, 1.0, 0.0).astype(BF)


def here():
    return lax.axis_index("help")


def has_previous():
    return lax.axis_index(SUB) > 0


def has_next():
    return lax.axis_index(SUB) + 1 < lax.axis_size(SUB)


def weight(flag):
    return flag.astype(jnp.int32).astype(F32)


def blocks_of(*blocks):
    return tuple((block, k, 0) for k, block in enumerate(blocks))


def pick_body(own_ref, a_ref, b_ref, c_ref, later_ref, wg_ref, pick_ref):
    rows = own_ref.shape[0]
    for ref, k, start in blocks_of(own_ref, a_ref, b_ref, c_ref):
        at = pl.multiple_of(lax.rem(here() + 4 - k, 4) * rows + start, 16)
        wg_ref[pl.ds(at, ref.shape[0]), :] = ref[...]
    choose = hot(later_ref[...] == iota((later_ref.shape[0], wg_ref.shape[0]), 1))
    pick_ref[...] = mm(choose, wg_ref[...]).astype(BF)


def numbers(shape, values):
    col = iota(shape, 1)
    info = jnp.zeros(shape, F32)
    for k, value in enumerate(values):
        info = jnp.where(col == k, value.astype(F32), info)
    return info.astype(BF)


def number(row, at):
    return jnp.sum(jnp.where(iota(row.shape, 1) == at, row, 0.0)).astype(jnp.int32)


def place(pieces, rows, panel, tables, out_ref):
    for ref, k, start in pieces:
        at = start
        stop = min(start + ref.shape[0], rows)
        while at < stop:
            slot = at // panel
            end = min((slot + 1) * panel, stop)
            to = tables[k][slot] * panel + at % panel
            out_ref[pl.ds(pl.multiple_of(to, 16), end - at), :] = ref[at - start : end - start, :]
            at = end


def tables_of(index, pieces, rows):
    tables = [[index[0], index[1], index[2]], None, None, None]
    for ref, k, start in pieces[1:]:
        if start + ref.shape[0] > rows:
            row = ref[rows - start : rows - start + 1, :].astype(F32)
            tables[k] = [number(row, j) for j in range(3)]
    return tables


def early_body(index, f_ref, wg_ref, z_ref, info_ref):
    z_ref[...] = mm(f_ref[:, : wg_ref.shape[0]], wg_ref[...])
    info_ref[...] = numbers(info_ref.shape, [index[0], index[1], index[2]])


def first_body(f_ref, early_ref, info_ref, halo_ref, z_ref):
    rows = early_ref.shape[0]
    owned = f_ref.shape[1] - halo_ref.shape[0]
    from_halo = mm(f_ref[:, owned:], halo_ref[...])
    z_ref[:rows, :] = (early_ref[...] - weight(has_previous()) * from_halo).astype(BF)
    z_ref[rows:, :] = info_ref[...]


def spread_body(
    count, index, own_ref, a_ref, b_ref, c_ref, later_ref, zg_ref, halo_ref, pick_ref, table_ref
):
    rows = own_ref.shape[0] - 16
    pieces = blocks_of(own_ref, a_ref, b_ref, c_ref)
    tables = tables_of(index, pieces, rows)
    place(pieces, rows, rows // 3, tables, zg_ref)
    for k in range(4):
        for j in range(3):
            table_ref[3 * k + j] = tables[k][j]
    halo = halo_ref.shape[0]
    owned = zg_ref.shape[0] - halo
    halo_ref[...] = zg_ref[owned:, :]
    later = later_ref[...]
    choose = hot((later == iota((halo, owned), 1)) & (later < count[0]))
    pick_ref[:halo, :] = mm(choose, zg_ref[:owned, :]).astype(BF)
    pick_ref[halo:, :] = numbers((16, zg_ref.shape[1]), [count[0] // 32, count[0] % 32])


def second_body(
    count, f_ref, zg_ref, ret_ref, zp_ref, bor_ref, wg_ref, map_ref, later_ref, z_ref, im_ref, vb_ref, vh_ref
):
    owned = wg_ref.shape[0]
    halo = ret_ref.shape[0]
    live = iota((owned, 1), 0) < count[0]
    back = mm(hot(iota((owned, halo), 0) == later_ref[...]), ret_ref[...])
    image = jnp.where(live, zg_ref[:owned, :].astype(F32) - weight(has_next()) * back, 0.0)
    im_ref[...] = image
    vb = (image - SHIFT * wg_ref[...].astype(F32)).astype(BF)
    vb_ref[...] = vb
    info = zp_ref[halo : halo + 1, :].astype(F32)
    lane = iota(info.shape, 1)
    parts = jnp.where(lane == 0, 32.0, jnp.where(lane == 1, 1.0, 0.0))
    before = jnp.sum(info * parts, axis=1, keepdims=True)
    alive = map_ref[...].astype(F32) < before
    term = zp_ref[:halo, :].astype(F32) - zg_ref[owned:, :].astype(F32)
    vh = jnp.where(alive, term, 0.0) - SHIFT * bor_ref[...].astype(F32)
    vh = (weight(has_previous()) * vh).astype(BF)
    vh_ref[...] = vh
    z = mm(f_ref[:, :owned], vb) - mm(f_ref[:, owned:], vh)
    z_ref[...] = z.astype(BF)


def gram_body(
    index, own_ref, a_ref, b_ref, c_ref, wg_ref, bor_ref, zg_ref, im_ref, vb_ref, vh_ref,
    keep_ref, give_ref, z2_ref, gram_ref, pack_ref,
):
    rows = own_ref.shape[0]
    tables = [[index[3 * k + j] for j in range(3)] for k in range(4)]
    place(blocks_of(own_ref, a_ref, b_ref, c_ref), rows, rows // 3, tables, z2_ref)
    owned = wg_ref.shape[0]
    h = here()

    @pl.when(h == 0)
    def _():
        gram_ref[...] = tmm(wg_ref[...], wg_ref[...])

    @pl.when(h == 1)
    def _():
        from_halo = tmm(bor_ref[...], zg_ref[owned:, :])
        gram_ref[...] = tmm(wg_ref[...], zg_ref[:owned, :]) - weight(has_previous()) * from_halo

    @pl.when(h == 2)
    def _():
        high, low = halves(im_ref[...])
        cross = tmm(low, high)
        gram_ref[...] = tmm(high, high) + (cross + cross.T)

    @pl.when(h == 3)
    def _():
        gram_ref[...] = tmm(vb_ref[...], z2_ref[:owned, :]) - tmm(vh_ref[...], z2_ref[owned:, :])

    half = gram_ref.shape[0] // 2
    lower = gram_ref[:half, :half]
    upper = gram_ref[half:, half:]
    r, c = iota((half, half), 0), iota((half, half), 1)
    diagonal = jnp.sum(jnp.where(r == c, upper, 0.0), axis=0, keepdims=True)
    pack_ref[0, :half, :] = jnp.where(r >= c, lower, upper.T)
    pack_ref[1, :half, :] = gram_ref[half:, :half]
    pack_ref[0, half:, :] = jnp.broadcast_to(diagonal, (8, half))
    pack_ref[1, half:, :] = jnp.zeros((8, half), F32)
    core = lax.axis_index("sub_2")
    keep_ref[...] = pack_ref[core]
    give_ref[...] = pack_ref[1 - core]


def tail_body(z_ref, map_ref, mine_ref, back_ref):
    rows = mine_ref.shape[0]
    halo = map_ref.shape[1]
    at = pl.multiple_of(here() * rows, rows)
    mine_ref[...] = z_ref[pl.ds(at, rows), :]
    choose = hot(iota((rows, halo), 0) + at == map_ref[...])
    back_ref[...] = mm(choose, z_ref[z_ref.shape[0] - halo :, :]).astype(BF)


def unpacked(pack, out_ref):
    half = pack.shape[2]
    r, c = iota((half, half), 0), iota((half, half), 1)
    both = pack[0, :half, :]
    flip = both.T
    side = pack[1, :half, :]
    out_ref[:half, :half] = jnp.where(r >= c, both, flip)
    out_ref[half:, half:] = jnp.where(r == c, pack[0, half : half + 1, :], jnp.where(r < c, both, flip))
    out_ref[half:, :half] = side
    out_ref[:half, half:] = side.T


def inverse(k, x_ref):
    n = k.shape[0]
    r, c = iota((n, n), 0), iota((n, n), 1)
    eye = jnp.where(r == c, 1.0, 0.0)
    on = jnp.where(r == c, k, 0.0)
    by_row = lax.rsqrt(jnp.sum(on, axis=1, keepdims=True))
    by_col = lax.rsqrt(jnp.sum(on, axis=0, keepdims=True))
    unit = k * by_row * by_col
    norm = jnp.max(jnp.sum(jnp.abs(unit), axis=0, keepdims=True), axis=1, keepdims=True)
    step = 2.0 / (1.0 + norm)
    high, low = halves(unit)
    x = 2.0 * eye - unit
    left = eye - mm(high, x.astype(BF))
    for _ in range(2):
        x = x + mm(x.astype(BF), left.astype(BF))
        xh, xl = halves(x)
        left = eye - (mm(high, xh) + (mm(high, xl) + mm(low, xh)))
    x_ref[...] = x + mm(x.astype(BF), left.astype(BF))

    def size(error):
        return jnp.max(jnp.sum(jnp.abs(error), axis=0, keepdims=True))

    @pl.when(jnp.logical_not(size(left) < 3e-3))
    def _():
        x_ref[...] = step * eye

        def more(state):
            return (state[0] < 60) & (state[1] > 1e-3)

        def improve(state):
            x = x_ref[...]
            left = eye - mmf(unit, x)
            x_ref[...] = x + mmf(x, left)
            return state[0] + 1, size(left)

        lax.while_loop(more, improve, (jnp.int32(0), jnp.float32(1.0)))

    return x_ref[...] * by_row * by_col


def solve_body(
    count, own_ref, other_ref, r_ref, im_ref, w_ref, mine_ref, ret_ref,
    sol_ref, res_ref, pack_ref, g00_ref, g01_ref, g11_ref, gvv_ref, x_ref,
):
    h = here()
    core = lax.axis_index("sub_2")
    for k in range(4):
        at = lax.rem(h + 4 - k, 4)
        pack_ref[at, core] = own_ref[k]
        pack_ref[at, 1 - core] = other_ref[k]
    for k, ref in enumerate((g00_ref, g01_ref, g11_ref, gvv_ref)):
        unpacked(pack_ref.at[k], ref)
    g01 = g01_ref[...]
    mixed = g11_ref[...] - SHIFT * g01
    inv = inverse(g01, x_ref)
    p1 = mm3(inv, mixed)
    p2 = mm3(inv, g00_ref[...])
    schur = gvv_ref[...] - mm3(mixed, p1)
    schur = 0.5 * (schur + schur.T)
    rest = g01 - SHIFT * g00_ref[...] - mm3(mixed, p2)
    cv = mm3(inverse(schur, x_ref), rest)
    cr = p2 - mm3(p1, cv)
    rows = r_ref.shape[0]
    live = iota((rows, 1), 0) + h * rows < count[0]
    r = jnp.where(live, r_ref[...], 0.0)
    at = pl.multiple_of(h * rows, rows)
    im = im_ref[pl.ds(at, rows), :]
    v = im - SHIFT * w_ref[...].astype(F32)
    av = jnp.where(live, mine_ref[...].astype(F32) - weight(has_next()) * ret_ref[...].astype(F32), 0.0)
    sol_ref[...] = mm3(r, cr) + mm3(v, cv)
    res_ref[...] = r - mm3(im, cr) - mm3(av, cv)


def shards(right_side, operator_panels, panel_index, halo_map, counts):
    rows, cols = right_side.shape[1:]
    slots, panel, wide = operator_panels.shape
    halo = halo_map.shape[1]
    half = cols // 2
    owned = rows * lax.axis_size("help")
    r = right_side.reshape(rows, cols)
    f = operator_panels.reshape(slots * panel, wide)
    later = turned(halo_map.reshape(halo), SUB, -1)
    later_col, later_row = later.reshape(halo, 1), later.reshape(1, halo)
    map_col, map_row = halo_map.reshape(halo, 1), halo_map.reshape(1, halo)

    row_ids = lax.axis_index("help") * rows + jnp.arange(rows, dtype=jnp.int32)
    low = jnp.where(row_ids[:, None] < counts, r, 0.0).astype(BF)
    wg, pick = call(
        pick_body,
        (low, *from_others(low, "help"), later_col),
        [((owned, cols), BF), ((halo, cols), BF)],
        small=0,
        name="pick",
    )
    bor = turned(pick, SUB, 1)
    early, info = call(
        early_body, (panel_index, f, wg), [((slots * panel, cols), F32), ((16, cols), BF)], name="early"
    )
    (z,) = call(
        first_body, (f, early, info, bor), [((slots * panel + 16, cols), BF)], small=0, name="first"
    )
    zg, zh, zpick, index = call(
        spread_body,
        (counts, panel_index, z, *from_others(z, "help"), later_col),
        [((wide, cols), BF), ((halo, cols), BF), ((halo + 16, cols), BF), ((12,), jnp.int32)],
        small=2,
        name="spread",
        tail=scalars(),
    )
    ret = turned(zh, SUB, -1)
    zp = turned(zpick, SUB, 1)
    z2, im, vb, vh = call(
        second_body,
        (counts, f, zg, ret, zp, bor, wg, map_col, later_row),
        [((slots * panel, cols), BF), ((owned, cols), F32), ((owned, cols), BF), ((halo, cols), BF)],
        name="second",
    )
    keep, give, z2g = call(
        gram_body,
        (index, z2, *from_others(z2, "help"), wg, bor, zg, im, vb, vh),
        [((half + 8, half), F32), ((half + 8, half), F32), ((wide, cols), BF)],
        scratch=[pltpu.VMEM((cols, cols), F32), pltpu.VMEM((2, half + 8, half), F32)],
        name="gram",
    )
    pack = keep + turned(give, "sub_2", 1)
    mine, back = call(
        tail_body, (z2g, map_row), [((rows, cols), BF), ((rows, cols), BF)], small=0, name="tail"
    )
    pack = summed(pack, "sub_0")
    pack, back = lax.optimization_barrier((pack, back))
    ret2 = turned(back, SUB, -1)
    pack = summed(pack, "sub_1")
    pack, ret2 = lax.optimization_barrier((pack, ret2))
    packs = jnp.stack([pack, *from_others(pack, "help")])
    sol, res = call(
        solve_body,
        (counts, packs, turned(packs, "sub_2", 1), r, im, low, mine, ret2),
        [((rows, cols), F32), ((rows, cols), F32)],
        scratch=[pltpu.VMEM((4, 2, half + 8, half), F32)] + [pltpu.VMEM((cols, cols), F32)] * 5,
        name="solve",
    )
    return sol.reshape(right_side.shape), res.reshape(right_side.shape)


def solution(mesh):
    torus = Mesh(
        mesh.devices.reshape(4, 4, 2, mesh.shape["help"]), ("sub_0", "sub_1", "sub_2", "help")
    )
    in_specs = (P(SUB, "help", None), P(SUB_HELP, None, None), P(SUB_HELP), P(SUB, None), P(SUB))
    out_specs = (P(SUB, "help", None), P(SUB, "help", None))
    return jax.shard_map(
        shards, mesh=torus, in_specs=in_specs, out_specs=out_specs, check_vma=False
    )
```
